512 devices in a mesh: gx: 64 (over x, z, core), gy: 8 (over y).
Axes of the slice: x: 4, y: 8, z: 8, core: 2. Of those that a mesh axis runs over, the one named last changes fastest.
Arguments:
- right_side: float32 [64, 16, 8, 8, 128], P('gx', 'gy'), may hold values from -6 to 6
- inverse_blocks: float32 [64, 16, 8, 128, 128], P('gx', 'gy'), may hold values from -1.7 to 1.7
- couple_x: float32 [64, 16, 8, 8, 128], P('gx', 'gy'), may hold values from -0.127 to -0.105
- couple_y: float32 [64, 16, 8, 8, 128], P('gx', 'gy'), may hold values from -0.007 to -0.003
- couple_z: float32 [64, 16, 8, 8, 8], P('gx', 'gy'), may hold values from -0.75 to 0.75
Outputs:
- solution: float32 [64, 16, 8, 8, 128], P('gx', 'gy')
The draws below stay inside these ranges and needn't reach their ends.
All inputs are finite; a program needn't handle non-finite values.
Results may differ from the reference program's by a relative error of at most 0.0001.
Values sent between devices are 32-bit elements; how exact they have to be, the bound alone decides.
No kernel may reach another device: no remote copies, remote signals or barrier semaphores. Data moves between devices by JAX's collectives and lax.ppermute only.
A program may use at most 64 MiB of HBM per device.

```python
import math
import jax
import jax.numpy as jnp
from jax import lax

NC = 8
ZB = 8
NRHS = 8
BR = 128
NZ = 128
NX = 64
NY = 16


def draw_inverse_blocks(key, part):
    key_diag, key_rest = jax.random.split(key)
    scales = jax.random.uniform(key_diag, (NX, NY, ZB, BR, 1), jnp.float32, 0.6, 1.4)
    spread = jax.random.normal(key_rest, (NX, NY, ZB, BR, BR), jnp.float32) * (0.35 / math.sqrt(BR))
    return spread + scales * jnp.eye(BR, dtype=jnp.float32)


def draw_couple_x(key, part):
    inner = jax.random.fold_in(key, 11)
    magnitude = jax.random.uniform(inner, (NX, NY, NC, NC, NZ), jnp.float32, 0.105, 0.127)
    return -magnitude


def draw_couple_y(key, part):
    inner = jax.random.fold_in(key, 23)
    magnitude = jax.random.uniform(inner, (NX, NY, NC, NC, NZ), jnp.float32, 0.003, 0.007)
    return -magnitude


def block_scale(key, extent, cuts, low, high):
    gain = 1.0
    for dim, shards_of in cuts:
        draws = jax.random.uniform(jax.random.fold_in(jax.random.fold_in(key, 6), dim), (shards_of,), jnp.float32, low / len(cuts), high / len(cuts))
        gain = gain * jnp.repeat(jnp.exp(draws), extent[dim] // shards_of).reshape((-1,) + (1,) * (len(extent) - 1 - dim))
    return gain


def centred(key, shape, deviation, most, cuts=(), held_as=jnp.bfloat16):
    gain = block_scale(key, shape, cuts, -0.22, 0.18) if cuts else 1.0
    result = jax.random.normal(key, shape, jnp.float32) * deviation * gain
    return jnp.minimum(jnp.maximum(result, -most), most).astype(held_as)


def setup_inputs(seed: int = 0) -> dict:
    streams_of = jax.random.split(jax.random.key(seed), 6)
    return {
        "right_side": centred(streams_of[0], (NX, NY, NRHS, NC, NZ), 1.0, 6.0, ((0, 64), (1, 8)), jnp.float32),
        "inverse_blocks": draw_inverse_blocks(jax.random.fold_in(streams_of[5], 71), 0),
        "couple_x": draw_couple_x(jax.random.fold_in(streams_of[5], 71), 0),
        "couple_y": draw_couple_y(jax.random.fold_in(streams_of[5], 71), 0),
        "couple_z": centred(streams_of[4], (NX, NY, ZB, NC, NC), 0.125, 0.75, ((0, 64), (1, 8)), jnp.float32),
    }


exact_mode = lax.Precision.HIGHEST


def couple(matrix, values_in):
    return jnp.einsum("cdz,ndz->ncz", matrix, values_in, precision=exact_mode)


def reference(right_side, inverse_blocks, couple_x, couple_y, couple_z):
    vectors = right_side.shape[2]
    components = right_side.shape[3]
    z_cells = right_side.shape[4]
    segments = inverse_blocks.shape[2]
    seg_len = z_cells // segments

    def segment_step(z_prior, inputs):
        seg_piece, inverse, corner = inputs
        head_row = seg_piece[:, :, 0] - jnp.einsum("cd,nd->nc", corner, z_prior, precision=exact_mode)
        seg_piece = jnp.concatenate([head_row[:, :, None], seg_piece[:, :, 1:]], axis=2)
        flattened = seg_piece.reshape(vectors, components * seg_len)
        solved = jnp.dot(flattened, inverse.T, precision=exact_mode, preferred_element_type=jnp.float32)
        solved = solved.reshape(vectors, components, seg_len)
        return solved[:, :, -1], solved

    def column_step(y_prior, inputs):
        partial_value, inverse, along_y, corner = inputs
        partial_value = partial_value - couple(along_y, y_prior)
        pieces = partial_value.reshape(vectors, components, segments, seg_len).transpose(2, 0, 1, 3)
        zero_state = jnp.zeros((vectors, components), jnp.float32)
        _, solved = lax.scan(segment_step, zero_state, (pieces, inverse, corner))
        column = solved.transpose(1, 2, 0, 3).reshape(vectors, components, z_cells)
        return column, column

    def plane_step(x_prior, inputs):
        rhs_plane, inverse, along_x, along_y, corner = inputs
        partial_value = rhs_plane - jnp.einsum("ycdz,yndz->yncz", along_x, x_prior, precision=exact_mode)
        zero_column = jnp.zeros((vectors, components, z_cells), jnp.float32)
        _, x_plane = lax.scan(column_step, zero_column, (partial_value, inverse, along_y, corner))
        return x_plane, x_plane

    zero_plane = jnp.zeros(right_side.shape[1:], jnp.float32)
    _, solution = lax.scan(plane_step, zero_plane, (right_side, inverse_blocks, couple_x, couple_y, couple_z))
    return solution
```

```python
import jax
import jax.numpy as jnp
from jax import lax
from jax.experimental import pallas as pl
from jax.experimental.pallas import tpu as pltpu
from jax.sharding import PartitionSpec as P

AXES = ("gx", "gy")
ROUNDS = 8
REPEAT = 9
VMEM = pl.BlockSpec(memory_space=pltpu.VMEM)
ANY = pl.BlockSpec(memory_space=pl.ANY)


def swap_groups(a):
    row = lax.broadcasted_iota(jnp.int32, a.shape, 0)
    group = lax.broadcasted_iota(jnp.int32, a.shape, 1) // 16
    ahead = (group - row) & 7
    out = a
    for d in range(1, 8):
        moved = pltpu.roll(pltpu.roll(a, 8 - d, 0), 16 * d, 1)
        out = jnp.where(ahead == d, moved, out)
    return out


def pack_kernel(rhs, inverse, cx, cy, cz, *rest):
    outs, small = rest[:4], rest[4]
    chip = lax.rem(lax.axis_index("gx"), ROUNDS) // 2
    row = lax.broadcasted_iota(jnp.int32, (8, 128), 0)
    group = lax.broadcasted_iota(jnp.int32, (8, 128), 1) // 16
    spread_row = lax.broadcasted_iota(jnp.int32, (8, 128), 0)
    spread_lane = lax.broadcasted_iota(jnp.int32, (8, 128), 1)
    spread = jnp.where(spread_lane == 16 * spread_row, 1.0, 0.0)
    heads = jnp.dot(
        cz[...], spread, precision=lax.Precision.HIGHEST, preferred_element_type=jnp.float32
    )
    for y in range(2):
        for n in range(8):
            small[y, :, n, :] = swap_groups(rhs[y, n])
        for ref, base in ((cx, 8), (cy, 16)):
            for m in range(8):
                a = ref[y, m]
                for c in range(8):
                    if c != m:
                        a = jnp.where(row == (c - m) % 8, ref[y, c], a)
                small[y, :, base + m, :] = swap_groups(a)
        for s in range(8):
            t = heads[(y * 8 + s) * 8 : (y * 8 + s + 1) * 8]
            out = t
            for d in range(1, 8):
                out = jnp.where(group == d, pltpu.roll(t, 8 - d, 0), out)
            small[y, s, 24:32, :] = out
    for q in range(4):
        first = 2 * (chip ^ q)
        for y in range(2):
            for k in range(2):
                outs[q][y * 2 + k, 0:128, :] = inverse[y, first + k].T
                outs[q][y * 2 + k, 128:160, :] = small[y, first + k]


def prepare_kernel(*refs):
    parts, weights, rows = refs[:ROUNDS], refs[ROUNDS], refs[ROUNDS + 1]
    place = lax.rem(lax.axis_index("gx"), ROUNDS)
    for r in range(ROUNDS):
        x = place ^ r
        for b in range(4):
            full = parts[r][b, 0:128, :]
            high = full.astype(jnp.bfloat16)
            low = (full - high.astype(jnp.float32)).astype(jnp.bfloat16)
            weights[x, b, :, 0:128] = high
            weights[x, b, :, 128:256] = low
            rows[x, b] = parts[r][b, 128:160, :]


def step_kernel(step, weights, rows, in_x, in_y, in_z, _, tile, out_x, out_y, out_z):
    gx, gy = lax.axis_index("gx"), lax.axis_index("gy")
    level = gx // ROUNDS + gy + lax.rem(gx, ROUNDS) // 2
    last_lane = lax.rem(lax.broadcasted_iota(jnp.int32, (8, 128), 1), 16) == 15

    @pl.when((level == step) & (lax.rem(gx, 2) == 0))
    def _():
        z_packed = in_z[...]

        def advance(i, carry):
            done, z_out = carry[:4], carry[4]
            new = []
            for y in range(2):
                for k in range(2):
                    b = y * 2 + k
                    x = i - y - k
                    inside = (x >= 0) & (x < ROUNDS)
                    xc = jnp.clip(x, 0, ROUNDS - 1)
                    from_x = done[b]
                    from_y = in_y[xc, k] if y == 0 else done[k]
                    if k == 0:
                        from_z = pltpu.roll(z_packed, lax.rem(128 - (xc * 2 + y), 128), 1)
                    else:
                        from_z = pltpu.roll(done[y * 2], 113, 1)
                    terms = []
                    for m in range(8):
                        q = (
                            rows[xc, b, 8 + m : 9 + m, :] * from_x
                            + rows[xc, b, 16 + m : 17 + m, :] * from_y
                            + rows[xc, b, 24 + m : 25 + m, :] * from_z
                        )
                        terms.append(pltpu.roll(q, 16 * m, 1) if m else q)
                    while len(terms) > 1:
                        terms = [u + v for u, v in zip(terms[::2], terms[1::2])]
                    partial = rows[xc, b, 0:8, :] - terms[0]
                    high = partial.astype(jnp.bfloat16).astype(jnp.float32)
                    both = jnp.concatenate([high, partial - high], axis=0).astype(jnp.bfloat16)
                    product = jnp.dot(
                        both, weights[xc, b], preferred_element_type=jnp.float32
                    )
                    solved = (product[0:8, 0:128] + product[8:16, 0:128]) + (
                        product[0:8, 128:256] + product[8:16, 128:256]
                    )
                    solved = jnp.where(inside, solved, done[b])
                    tile[xc, b] = solved
                    if y == 1:
                        out_y[xc, k] = solved
                    if k == 1:
                        kept = jnp.where(last_lane & inside, solved, 0.0)
                        z_out = z_out + pltpu.roll(kept, lax.rem(xc * 2 + y + 113, 128), 1)
                    new.append(solved)
            return (*new, z_out)

        carry = tuple(in_x[b] for b in range(4)) + (jnp.zeros((8, 128), jnp.float32),)
        carry = lax.fori_loop(0, ROUNDS + 2, advance, carry)
        for b in range(4):
            out_x[b] = carry[b]
        out_z[...] = carry[4]


def unpack_kernel(parts, out):
    for y in range(2):
        for n in range(8):
            rows = jnp.concatenate(
                [parts[2 * (s // 2), y * 2 + s % 2, n : n + 1, :] for s in range(8)], axis=0
            )
            out[y, n] = swap_groups(rows)


def f32(*shape):
    return jax.ShapeDtypeStruct(shape, jnp.float32)


def tile_level(gx, gy):
    return gx // ROUNDS + gy + gx % ROUNDS // 2


def local(right_side, inverse_blocks, couple_x, couple_y, couple_z):
    nx, ny = lax.axis_size("gx"), lax.axis_size("gy")
    outs = pl.pallas_call(
        pack_kernel,
        out_shape=[f32(4, 160, 128)] * 4,
        in_specs=[VMEM] * 5,
        out_specs=[VMEM] * 4,
        scratch_shapes=[pltpu.VMEM((2, 8, 32, 128), jnp.float32)],
        compiler_params=pltpu.CompilerParams(vmem_limit_bytes=12 << 20),
        name="pack",
    )(
        right_side[0],
        inverse_blocks[0],
        couple_x[0],
        couple_y[0],
        couple_z.reshape(128, 8),
    )

    def device(gx, gy):
        return gx * ny + gy

    parts = [outs[0]]
    for r in range(1, ROUNDS):
        pairs = [
            (device(gx, gy), device(gx ^ r, gy))
            for gx in range(nx)
            for gy in range(ny)
            if (gx ^ r) % 2 == 0
        ]
        parts.append(lax.ppermute(outs[r // 2], AXES, pairs))
    weights, rows = pl.pallas_call(
        prepare_kernel,
        out_shape=[
            jax.ShapeDtypeStruct((ROUNDS, 4, 128, 256), jnp.bfloat16),
            f32(ROUNDS, 4, 32, 128),
        ],
        in_specs=[VMEM] * ROUNDS,
        out_specs=[VMEM] * 2,
        compiler_params=pltpu.CompilerParams(vmem_limit_bytes=16 << 20),
        name="prepare",
    )(*parts)

    steps = nx // ROUNDS + ny + 4 - 2
    tile = jnp.zeros((ROUNDS, 4, 8, 128), jnp.float32)
    in_x = jnp.zeros((4, 8, 128), jnp.float32)
    in_y = jnp.zeros((ROUNDS, 2, 8, 128), jnp.float32)
    in_z = jnp.zeros((8, 128), jnp.float32)
    for step in range(steps):
        def body(*refs, step=step):
            step_kernel(step, *refs)

        tile, out_x, out_y, out_z = pl.pallas_call(
            body,
            out_shape=[
                f32(ROUNDS, 4, 8, 128),
                f32(4, 8, 128),
                f32(ROUNDS, 2, 8, 128),
                f32(8, 128),
            ],
            in_specs=[VMEM] * 6,
            out_specs=[VMEM] * 4,
            input_output_aliases={5: 0},
            compiler_params=pltpu.CompilerParams(vmem_limit_bytes=12 << 20),
            name=f"tile_step",
        )(weights, rows, in_x, in_y, in_z, tile)
        if step == steps - 1:
            break
        tiles = [
            (gx, gy)
            for gx in range(0, nx, 2)
            for gy in range(ny)
            if tile_level(gx, gy) % REPEAT == step % REPEAT
        ]
        to_x = [(device(gx, gy), device(gx + ROUNDS, gy)) for gx, gy in tiles if gx + ROUNDS < nx]
        to_y = [(device(gx, gy), device(gx, gy + 1)) for gx, gy in tiles if gy + 1 < ny]
        to_z = [(device(gx, gy), device(gx + 2, gy)) for gx, gy in tiles if gx % ROUNDS + 2 < ROUNDS]
        in_x = lax.ppermute(out_x, AXES, to_x)
        in_y = lax.ppermute(out_y, AXES, to_y)
        in_z = lax.ppermute(out_z, AXES, to_z)

    groups = [list(range(g, g + ROUNDS)) for g in range(0, nx, ROUNDS)]
    parts = lax.all_to_all(tile, "gx", 0, 0, axis_index_groups=groups, tiled=True)
    result = pl.pallas_call(
        unpack_kernel,
        out_shape=f32(2, 8, 8, 128),
        in_specs=[VMEM],
        out_specs=VMEM,
        name="unpack",
    )(parts)
    return result[None]


def solution(mesh):
    spec = P("gx", "gy", None, None, None)
    return jax.shard_map(
        local, mesh=mesh, in_specs=(spec,) * 5, out_specs=spec, check_vma=False
    )
```

```python
import jax
import jax.numpy as jnp
from jax import lax
from jax.experimental import pallas as pl
from jax.experimental.pallas import tpu as pltpu
from jax.sharding import PartitionSpec as P

AXES = ("gx", "gy")
ROUNDS = 8
REPEAT = 9
VMEM = pl.BlockSpec(memory_space=pltpu.VMEM)
HBM = pl.BlockSpec(memory_space=pltpu.HBM)


def swap_groups(a):
    row = lax.broadcasted_iota(jnp.int32, a.shape, 0)
    group = lax.broadcasted_iota(jnp.int32, a.shape, 1) // 16
    ahead = (group - row) & 7
    out = a
    for d in range(1, 8):
        moved = pltpu.roll(pltpu.roll(a, 8 - d, 0), 16 * d, 1)
        out = jnp.where(ahead == d, moved, out)
    return out


def pack_kernel(*refs):
    sources, outs, small, held, arrived = refs[:5], refs[5:9], refs[9], refs[10:15], refs[15]
    copies = [
        pltpu.make_async_copy(source, target, arrived.at[i])
        for i, (source, target) in enumerate(zip(sources, held))
    ]
    for copy in copies:
        copy.start()
    for copy in copies:
        copy.wait()
    rhs, inverse, cx, cy, cz = held
    chip = lax.rem(lax.axis_index("gx"), ROUNDS) // 2
    row = lax.broadcasted_iota(jnp.int32, (8, 128), 0)
    group = lax.broadcasted_iota(jnp.int32, (8, 128), 1) // 16
    spread_row = lax.broadcasted_iota(jnp.int32, (8, 128), 0)
    spread_lane = lax.broadcasted_iota(jnp.int32, (8, 128), 1)
    spread = jnp.where(spread_lane == 16 * spread_row, 1.0, 0.0)
    heads = jnp.dot(
        cz[...], spread, precision=lax.Precision.HIGHEST, preferred_element_type=jnp.float32
    )
    for y in range(2):
        for n in range(8):
            small[y, :, n, :] = swap_groups(rhs[y, n])
        for ref, base in ((cx, 8), (cy, 16)):
            for m in range(8):
                a = ref[y, m]
                for c in range(8):
                    if c != m:
                        a = jnp.where(row == (c - m) % 8, ref[y, c], a)
                small[y, :, base + m, :] = swap_groups(a)
        for s in range(8):
            t = heads[(y * 8 + s) * 8 : (y * 8 + s + 1) * 8]
            out = t
            for d in range(1, 8):
                out = jnp.where(group == d, pltpu.roll(t, 8 - d, 0), out)
            small[y, s, 24:32, :] = out
    for q in range(4):
        first = 2 * (chip ^ q)
        for y in range(2):
            for k in range(2):
                outs[q][y * 2 + k, 0:128, :] = inverse[y, first + k].T
                outs[q][y * 2 + k, 128:160, :] = small[y, first + k]


def prepare_kernel(*refs):
    parts, weights, rows = refs[:ROUNDS], refs[ROUNDS], refs[ROUNDS + 1]
    place = lax.rem(lax.axis_index("gx"), ROUNDS)
    for r in range(ROUNDS):
        x = place ^ r
        for b in range(4):
            full = parts[r][b, 0:128, :]
            high = full.astype(jnp.bfloat16)
            low = (full - high.astype(jnp.float32)).astype(jnp.bfloat16)
            weights[x, b, :, 0:128] = high
            weights[x, b, :, 128:256] = low
            rows[x, b] = parts[r][b, 128:160, :]


def step_kernel(step, weights, rows, in_x, in_y, in_z, _, tile, out_x, out_y, out_z):
    gx, gy = lax.axis_index("gx"), lax.axis_index("gy")
    level = gx // ROUNDS + gy + lax.rem(gx, ROUNDS) // 2
    last_lane = lax.rem(lax.broadcasted_iota(jnp.int32, (8, 128), 1), 16) == 15

    @pl.when((level == step) & (lax.rem(gx, 2) == 0))
    def _():
        z_packed = in_z[...]

        done = [in_x[b] for b in range(4)]
        z_out = jnp.zeros((8, 128), jnp.float32)
        for i in range(ROUNDS + 2):
            before = list(done)
            for y in range(2):
                for k in range(2):
                    b, x = y * 2 + k, i - y - k
                    if not 0 <= x < ROUNDS:
                        continue
                    from_y = in_y[x, k] if y == 0 else before[k]
                    if k == 0:
                        place = x * 2 + y
                        from_z = pltpu.roll(z_packed, 128 - place, 1) if place else z_packed
                    else:
                        from_z = pltpu.roll(before[y * 2], 113, 1)
                    terms = []
                    for m in range(8):
                        q = (
                            rows[x, b, 8 + m : 9 + m, :] * before[b]
                            + rows[x, b, 16 + m : 17 + m, :] * from_y
                            + rows[x, b, 24 + m : 25 + m, :] * from_z
                        )
                        terms.append(pltpu.roll(q, 16 * m, 1) if m else q)
                    while len(terms) > 1:
                        terms = [u + v for u, v in zip(terms[::2], terms[1::2])]
                    partial = rows[x, b, 0:8, :] - terms[0]
                    high = partial.astype(jnp.bfloat16).astype(jnp.float32)
                    both = jnp.concatenate([high, partial - high], axis=0).astype(jnp.bfloat16)
                    product = jnp.dot(both, weights[x, b], preferred_element_type=jnp.float32)
                    solved = (product[0:8, 0:128] + product[8:16, 0:128]) + (
                        product[0:8, 128:256] + product[8:16, 128:256]
                    )
                    tile[x, b] = solved
                    done[b] = solved
                    if y == 1:
                        out_y[x, k] = solved
                    if k == 1:
                        kept = jnp.where(last_lane, solved, 0.0)
                        z_out = z_out + pltpu.roll(kept, (x * 2 + y + 113) % 128, 1)
        for b in range(4):
            out_x[b] = done[b]
        out_z[...] = z_out


def unpack_kernel(parts, out):
    for y in range(2):
        for n in range(8):
            rows = jnp.concatenate(
                [parts[2 * (s // 2), y * 2 + s % 2, n : n + 1, :] for s in range(8)], axis=0
            )
            out[y, n] = swap_groups(rows)


def f32(*shape):
    return jax.ShapeDtypeStruct(shape, jnp.float32)


def tile_level(gx, gy):
    return gx // ROUNDS + gy + gx % ROUNDS // 2


def local(right_side, inverse_blocks, couple_x, couple_y, couple_z):
    nx, ny = lax.axis_size("gx"), lax.axis_size("gy")
    outs = pl.pallas_call(
        pack_kernel,
        out_shape=[f32(4, 160, 128)] * 4,
        in_specs=[HBM] * 5,
        out_specs=[VMEM] * 4,
        scratch_shapes=[
            pltpu.VMEM((2, 8, 32, 128), jnp.float32),
            pltpu.VMEM((2, 8, 8, 128), jnp.float32),
            pltpu.VMEM((2, 8, 128, 128), jnp.float32),
            pltpu.VMEM((2, 8, 8, 128), jnp.float32),
            pltpu.VMEM((2, 8, 8, 128), jnp.float32),
            pltpu.VMEM((128, 8), jnp.float32),
            pltpu.SemaphoreType.DMA((5,)),
        ],
        compiler_params=pltpu.CompilerParams(vmem_limit_bytes=12 << 20),
        name="pack",
    )(
        right_side[0],
        inverse_blocks[0],
        couple_x[0],
        couple_y[0],
        couple_z.reshape(128, 8),
    )

    def device(gx, gy):
        return gx * ny + gy

    parts = [outs[0]]
    for r in range(1, ROUNDS):
        pairs = [
            (device(gx, gy), device(gx ^ r, gy))
            for gx in range(nx)
            for gy in range(ny)
            if (gx ^ r) % 2 == 0
        ]
        parts.append(lax.ppermute(outs[r // 2], AXES, pairs))
    weights, rows = pl.pallas_call(
        prepare_kernel,
        out_shape=[
            jax.ShapeDtypeStruct((ROUNDS, 4, 128, 256), jnp.bfloat16),
            f32(ROUNDS, 4, 32, 128),
        ],
        in_specs=[VMEM] * ROUNDS,
        out_specs=[VMEM] * 2,
        compiler_params=pltpu.CompilerParams(vmem_limit_bytes=16 << 20),
        name="prepare",
    )(*parts)

    steps = nx // ROUNDS + ny + 4 - 2
    tile = jnp.zeros((ROUNDS, 4, 8, 128), jnp.float32)
    in_x = jnp.zeros((4, 8, 128), jnp.float32)
    in_y = jnp.zeros((ROUNDS, 2, 8, 128), jnp.float32)
    in_z = jnp.zeros((8, 128), jnp.float32)
    for step in range(steps):
        def body(*refs, step=step):
            step_kernel(step, *refs)

        tile, out_x, out_y, out_z = pl.pallas_call(
            body,
            out_shape=[
                f32(ROUNDS, 4, 8, 128),
                f32(4, 8, 128),
                f32(ROUNDS, 2, 8, 128),
                f32(8, 128),
            ],
            in_specs=[VMEM] * 6,
            out_specs=[VMEM] * 4,
            input_output_aliases={5: 0},
            compiler_params=pltpu.CompilerParams(vmem_limit_bytes=12 << 20),
            name="tile_step",
        )(weights, rows, in_x, in_y, in_z, tile)
        if step == steps - 1:
            break
        tiles = [
            (gx, gy)
            for gx in range(0, nx, 2)
            for gy in range(ny)
            if tile_level(gx, gy) % REPEAT == step % REPEAT
        ]
        to_x = [(device(gx, gy), device(gx + ROUNDS, gy)) for gx, gy in tiles if gx + ROUNDS < nx]
        to_y = [(device(gx, gy), device(gx, gy + 1)) for gx, gy in tiles if gy + 1 < ny]
        to_z = [(device(gx, gy), device(gx + 2, gy)) for gx, gy in tiles if gx % ROUNDS + 2 < ROUNDS]
        in_x = lax.ppermute(out_x, AXES, to_x)
        in_y = lax.ppermute(out_y, AXES, to_y)
        in_z = lax.ppermute(out_z, AXES, to_z)

    groups = [list(range(g, g + ROUNDS)) for g in range(0, nx, ROUNDS)]
    parts = lax.all_to_all(tile, "gx", 0, 0, axis_index_groups=groups, tiled=True)
    result = pl.pallas_call(
        unpack_kernel,
        out_shape=f32(2, 8, 8, 128),
        in_specs=[VMEM],
        out_specs=VMEM,
        name="unpack",
    )(parts)
    return result[None]


def solution(mesh):
    spec = P("gx", "gy", None, None, None)
    return jax.shard_map(
        local, mesh=mesh, in_specs=(spec,) * 5, out_specs=spec, check_vma=False
    )
```

```python
import jax
import jax.numpy as jnp
from jax import lax
from jax.experimental import pallas as pl
from jax.experimental.pallas import tpu as pltpu
from jax.sharding import PartitionSpec as P

AXES = ("gx", "gy")
TILE_X = 8
TILE_Y = 4
ROUNDS = 16
OWNERS = (2, 4)
REPEAT = 6
VMEM = pl.BlockSpec(memory_space=pltpu.VMEM)
HBM = pl.BlockSpec(memory_space=pltpu.HBM)


def swap_groups(a):
    row = lax.broadcasted_iota(jnp.int32, a.shape, 0)
    group = lax.broadcasted_iota(jnp.int32, a.shape, 1) // 16
    ahead = (group - row) & 7
    out = a
    for d in range(1, 8):
        moved = pltpu.roll(pltpu.roll(a, 8 - d, 0), 16 * d, 1)
        out = jnp.where(ahead == d, moved, out)
    return out


def pack_kernel(*refs):
    sources, outs, small, held, arrived = refs[:5], refs[5:9], refs[9], refs[10:15], refs[15]
    copies = [
        pltpu.make_async_copy(source, target, arrived.at[i])
        for i, (source, target) in enumerate(zip(sources, held))
    ]
    for copy in copies:
        copy.start()
    for copy in copies:
        copy.wait()
    rhs, inverse, cx, cy, cz = held
    right = lax.rem(lax.axis_index("gx"), TILE_X) // 4
    upper = lax.rem(lax.axis_index("gy"), 2)
    row = lax.broadcasted_iota(jnp.int32, (8, 128), 0)
    group = lax.broadcasted_iota(jnp.int32, (8, 128), 1) // 16
    spread_row = lax.broadcasted_iota(jnp.int32, (8, 128), 0)
    spread_lane = lax.broadcasted_iota(jnp.int32, (8, 128), 1)
    spread = jnp.where(spread_lane == 16 * spread_row, 1.0, 0.0)
    heads = jnp.dot(
        cz[...], spread, precision=lax.Precision.HIGHEST, preferred_element_type=jnp.float32
    )
    for y in range(2):
        for n in range(8):
            small[y, :, n, :] = swap_groups(rhs[y, n])
        for ref, base in ((cx, 8), (cy, 16)):
            for m in range(8):
                a = ref[y, m]
                for c in range(8):
                    if c != m:
                        a = jnp.where(row == (c - m) % 8, ref[y, c], a)
                small[y, :, base + m, :] = swap_groups(a)
        for s in range(8):
            t = heads[(y * 8 + s) * 8 : (y * 8 + s + 1) * 8]
            out = t
            for d in range(1, 8):
                out = jnp.where(group == d, pltpu.roll(t, 8 - d, 0), out)
            small[y, s, 24:32, :] = out
    for q in range(4):
        first = 4 * (upper ^ (q // 2)) + 2 * (right ^ (q % 2))
        for y in range(2):
            for k in range(2):
                outs[q][y * 2 + k, 0:128, :] = inverse[y, first + k].T
                outs[q][y * 2 + k, 128:160, :] = small[y, first + k]


def prepare_kernel(*refs):
    parts, weights, rows = refs[:ROUNDS], refs[ROUNDS], refs[ROUNDS + 1]
    place = lax.rem(lax.axis_index("gx"), TILE_X)
    upper = lax.rem(lax.axis_index("gy"), 2)
    for r in range(ROUNDS):
        x, half = place ^ (r % TILE_X), upper ^ (r // TILE_X)
        for b in range(4):
            full = parts[r][b, 0:128, :]
            high = full.astype(jnp.bfloat16)
            low = (full - high.astype(jnp.float32)).astype(jnp.bfloat16)
            weights[x, half, b, :, 0:128] = high
            weights[x, half, b, :, 128:256] = low
            rows[x, half, b] = parts[r][b, 128:160, :]


def tile_level(gx, gy):
    return gx // TILE_X + gy // 2 + 2 * (gy % 2) + (gx % TILE_X) // 4


def step_kernel(step, weights, rows, in_x, in_y, in_z, _, tile, out_x, out_y, out_z):
    gx, gy = lax.axis_index("gx"), lax.axis_index("gy")
    place = lax.rem(gx, TILE_X)
    owner = (place == OWNERS[0]) | (place == OWNERS[1])
    level = gx // TILE_X + gy // 2 + 2 * lax.rem(gy, 2) + place // 4
    last_lane = lax.rem(lax.broadcasted_iota(jnp.int32, (8, 128), 1), 16) == 15

    @pl.when(owner & (level == step))
    def _():
        z_in = [in_z[h] for h in range(2)]
        z_out = [jnp.zeros((8, 128), jnp.float32) for h in range(2)]
        done = [in_x[b] for b in range(2 * TILE_Y)]
        for i in range(TILE_X + TILE_Y):
            before = list(done)
            for y in range(TILE_Y):
                for k in range(2):
                    b, x = y * 2 + k, i - y - k
                    if not 0 <= x < TILE_X:
                        continue
                    half, j = b // 4, b % 4
                    word, lane = (x * TILE_Y + y) // 16, (x * TILE_Y + y) % 16
                    from_y = in_y[x, k] if y == 0 else before[b - 2]
                    if k == 1:
                        from_z = pltpu.roll(before[b - 1], 113, 1)
                    else:
                        from_z = pltpu.roll(z_in[word], 128 - lane, 1) if lane else z_in[word]
                    terms = []
                    for m in range(8):
                        q = (
                            rows[x, half, j, 8 + m : 9 + m, :] * before[b]
                            + rows[x, half, j, 16 + m : 17 + m, :] * from_y
                            + rows[x, half, j, 24 + m : 25 + m, :] * from_z
                        )
                        terms.append(pltpu.roll(q, 16 * m, 1) if m else q)
                    while len(terms) > 1:
                        terms = [u + v for u, v in zip(terms[::2], terms[1::2])]
                    partial = rows[x, half, j, 0:8, :] - terms[0]
                    high = partial.astype(jnp.bfloat16).astype(jnp.float32)
                    both = jnp.concatenate([high, partial - high], axis=0).astype(jnp.bfloat16)
                    product = jnp.dot(
                        both, weights[x, half, j], preferred_element_type=jnp.float32
                    )
                    solved = (product[0:8, 0:128] + product[8:16, 0:128]) + (
                        product[0:8, 128:256] + product[8:16, 128:256]
                    )
                    tile[x, half, j] = solved
                    done[b] = solved
                    if y == TILE_Y - 1:
                        out_y[x, k] = solved
                    if k == 1:
                        kept = jnp.where(last_lane, solved, 0.0)
                        z_out[word] = z_out[word] + pltpu.roll(kept, (lane + 113) % 128, 1)
        for b in range(2 * TILE_Y):
            out_x[b] = done[b]
        for h in range(2):
            out_z[h] = z_out[h]


def unpack_kernel(parts, out):
    for y in range(2):
        for n in range(8):
            rows = jnp.concatenate(
                [
                    parts[2 * OWNERS[s // 2 % 2] + s // 4, y * 2 + s % 2, n : n + 1, :]
                    for s in range(8)
                ],
                axis=0,
            )
            out[y, n] = swap_groups(rows)


def f32(*shape):
    return jax.ShapeDtypeStruct(shape, jnp.float32)


def local(right_side, inverse_blocks, couple_x, couple_y, couple_z):
    nx, ny = lax.axis_size("gx"), lax.axis_size("gy")
    outs = pl.pallas_call(
        pack_kernel,
        out_shape=[f32(4, 160, 128)] * 4,
        in_specs=[HBM] * 5,
        out_specs=[VMEM] * 4,
        scratch_shapes=[
            pltpu.VMEM((2, 8, 32, 128), jnp.float32),
            pltpu.VMEM((2, 8, 8, 128), jnp.float32),
            pltpu.VMEM((2, 8, 128, 128), jnp.float32),
            pltpu.VMEM((2, 8, 8, 128), jnp.float32),
            pltpu.VMEM((2, 8, 8, 128), jnp.float32),
            pltpu.VMEM((128, 8), jnp.float32),
            pltpu.SemaphoreType.DMA((5,)),
        ],
        compiler_params=pltpu.CompilerParams(vmem_limit_bytes=12 << 20),
        name="pack",
    )(
        *(
            pltpu.with_memory_space_constraint(source, pltpu.HBM)
            for source in (
                right_side[0],
                inverse_blocks[0],
                couple_x[0],
                couple_y[0],
                couple_z.reshape(128, 8),
            )
        )
    )

    def device(gx, gy):
        return gx * ny + gy

    owners = [(gx, gy) for gx in range(nx) for gy in range(ny) if gx % TILE_X in OWNERS]
    parts = [outs[0]]
    for r in range(1, ROUNDS):
        across, along = r // TILE_X, r % TILE_X
        pairs = [(device(gx ^ along, gy ^ across), device(gx, gy)) for gx, gy in owners]
        parts.append(lax.ppermute(outs[2 * across + along // 4], AXES, pairs))
    weights, rows = pl.pallas_call(
        prepare_kernel,
        out_shape=[
            jax.ShapeDtypeStruct((TILE_X, 2, 4, 128, 256), jnp.bfloat16),
            f32(TILE_X, 2, 4, 32, 128),
        ],
        in_specs=[VMEM] * ROUNDS,
        out_specs=[VMEM] * 2,
        compiler_params=pltpu.CompilerParams(vmem_limit_bytes=16 << 20),
        name="prepare",
    )(*parts)

    steps = nx // TILE_X + ny // 2 + 4 - 2
    tile = jnp.zeros((TILE_X, 2, 4, 8, 128), jnp.float32)
    in_x = jnp.zeros((2 * TILE_Y, 8, 128), jnp.float32)
    in_y = jnp.zeros((TILE_X, 2, 8, 128), jnp.float32)
    in_z = jnp.zeros((2, 8, 128), jnp.float32)
    for step in range(steps):

        def body(*refs, step=step):
            step_kernel(step, *refs)

        tile, out_x, out_y, out_z = pl.pallas_call(
            body,
            out_shape=[f32(*tile.shape), f32(*in_x.shape), f32(*in_y.shape), f32(*in_z.shape)],
            in_specs=[VMEM] * 6,
            out_specs=[VMEM] * 4,
            input_output_aliases={5: 0},
            compiler_params=pltpu.CompilerParams(vmem_limit_bytes=12 << 20),
            name="tile_step",
        )(weights, rows, in_x, in_y, in_z, tile)
        if step == steps - 1:
            break
        to_x, to_y, to_z = [], [], []
        for gx, gy in owners:
            if tile_level(gx, gy) % REPEAT != step % REPEAT:
                continue
            here = device(gx, gy)
            if gx + TILE_X < nx:
                to_x.append((here, device(gx + TILE_X, gy)))
            if gy + 2 < ny:
                to_y.append((here, device(gx, gy + 2)))
            if gx % TILE_X == OWNERS[0]:
                to_z.append((here, device(gx + 2, gy)))
            elif gy % 2 == 0:
                to_z.append((here, device(gx - 2, gy + 1)))
        in_x = lax.ppermute(out_x, AXES, to_x)
        in_y = lax.ppermute(out_y, AXES, to_y)
        in_z = lax.ppermute(out_z, AXES, to_z)

    groups = [
        [device(gx + i, gy + j) for i in range(TILE_X) for j in range(2)]
        for gx in range(0, nx, TILE_X)
        for gy in range(0, ny, 2)
    ]
    parts = lax.all_to_all(
        tile.reshape(ROUNDS, 4, 8, 128), AXES, 0, 0, axis_index_groups=groups, tiled=True
    )
    result = pl.pallas_call(
        unpack_kernel,
        out_shape=f32(2, 8, 8, 128),
        in_specs=[VMEM],
        out_specs=VMEM,
        name="unpack",
    )(parts)
    return result[None]


def solution(mesh):
    spec = P("gx", "gy", None, None, None)
    return jax.shard_map(
        local, mesh=mesh, in_specs=(spec,) * 5, out_specs=spec, check_vma=False
    )
```

```python
import jax
import jax.numpy as jnp
from jax import lax
from jax.experimental import pallas as pl
from jax.experimental.pallas import tpu as pltpu
from jax.sharding import PartitionSpec as P

AXES = ("gx", "gy")
TILE_X = 8
TILE_Y = 4
MEMBERS = 16
ROUNDS = ((0, 0), (1, 0), (0, 1), (1, 1), (0, 2), (1, 2), (0, 3), (1, 3))
OWNERS = (2, 4)
REPEAT = 8
VMEM = pl.BlockSpec(memory_space=pltpu.VMEM)
HBM = pl.BlockSpec(memory_space=pltpu.HBM)


def swap_groups(a):
    row = lax.broadcasted_iota(jnp.int32, a.shape, 0)
    group = lax.broadcasted_iota(jnp.int32, a.shape, 1) // 16
    ahead = (group - row) & 7
    out = a
    for d in range(1, 8):
        moved = pltpu.roll(pltpu.roll(a, 8 - d, 0), 16 * d, 1)
        out = jnp.where(ahead == d, moved, out)
    return out


def pack_kernel(*refs):
    sources, outs, small, held, arrived = refs[:5], refs[5:8], refs[8], refs[9:14], refs[14]
    copies = [
        pltpu.make_async_copy(source, target, arrived.at[i])
        for i, (source, target) in enumerate(zip(sources, held))
    ]
    for copy in copies:
        copy.start()
    for copy in copies:
        copy.wait()
    rhs, inverse, cx, cy, cz = held
    gx = lax.axis_index("gx")
    core = lax.rem(gx, 2)
    pair = (lax.rem(gx, TILE_X) // 4) ^ lax.rem(gx // TILE_X, 2)
    upper = lax.rem(lax.axis_index("gy"), 2)
    row = lax.broadcasted_iota(jnp.int32, (8, 128), 0)
    group = lax.broadcasted_iota(jnp.int32, (8, 128), 1) // 16
    spread_row = lax.broadcasted_iota(jnp.int32, (8, 128), 0)
    spread_lane = lax.broadcasted_iota(jnp.int32, (8, 128), 1)
    spread = jnp.where(spread_lane == 16 * spread_row, 1.0, 0.0)
    heads = jnp.dot(
        cz[...], spread, precision=lax.Precision.HIGHEST, preferred_element_type=jnp.float32
    )
    for y in range(2):
        for n in range(8):
            small[y, :, n, :] = swap_groups(rhs[y, n])
        for ref, base in ((cx, 8), (cy, 16)):
            for m in range(8):
                a = ref[y, m]
                for c in range(8):
                    if c != m:
                        a = jnp.where(row == (c - m) % 8, ref[y, c], a)
                small[y, :, base + m, :] = swap_groups(a)
        for s in range(8):
            t = heads[(y * 8 + s) * 8 : (y * 8 + s + 1) * 8]
            out = t
            for d in range(1, 8):
                out = jnp.where(group == d, pltpu.roll(t, 8 - d, 0), out)
            small[y, s, 24:32, :] = out
    for across in range(2):
        for given in range(2):
            out = outs[2].at[across] if given else outs[across]
            first = 4 * (upper ^ across) + 2 * (pair ^ core ^ given)
            for y in range(2):
                for k in range(2):
                    out[y * 2 + k, 0:128, :] = inverse[y, first + k].T
                    out[y * 2 + k, 128:160, :] = small[y, first + k]


def prepare_kernel(*refs):
    parts, (weights, rows) = refs[: len(ROUNDS)], refs[len(ROUNDS) :]
    chip = lax.rem(lax.axis_index("gx"), TILE_X) // 2
    upper = lax.rem(lax.axis_index("gy"), 2)
    for part, (across, along) in zip(parts, ROUNDS):
        for i in range(2):
            x, half = 2 * (chip ^ along) + (i ^ (along // 2)), upper ^ across
            for b in range(4):
                full = part[i, b, 0:128, :]
                high = full.astype(jnp.bfloat16)
                low = (full - high.astype(jnp.float32)).astype(jnp.bfloat16)
                weights[x, half, b, :, 0:128] = high
                weights[x, half, b, :, 128:256] = low
                rows[x, half, b] = part[i, b, 128:160, :]


def tile_level(gx, gy):
    return gx // TILE_X + gy // 2 + 2 * (gy % 2) + ((gx % TILE_X) // 4 ^ (gx // TILE_X % 2))


def step_kernel(step, weights, rows, in_x, in_y, in_z, _, tile, out_x, out_y, out_z):
    gx, gy = lax.axis_index("gx"), lax.axis_index("gy")
    place = lax.rem(gx, TILE_X)
    owner = (place == OWNERS[0]) | (place == OWNERS[1])
    pair = (place // 4) ^ lax.rem(gx // TILE_X, 2)
    level = gx // TILE_X + gy // 2 + 2 * lax.rem(gy, 2) + pair
    last_lane = lax.rem(lax.broadcasted_iota(jnp.int32, (8, 128), 1), 16) == 15

    @pl.when(owner & (level == step))
    def _():
        z_in = [in_z[h] for h in range(2)]
        z_out = [jnp.zeros((8, 128), jnp.float32) for h in range(2)]
        done = [in_x[b] for b in range(2 * TILE_Y)]
        for i in range(TILE_X + TILE_Y):
            before = list(done)
            for y in range(TILE_Y):
                for k in range(2):
                    b, x = y * 2 + k, i - y - k
                    if not 0 <= x < TILE_X:
                        continue
                    half, j = b // 4, b % 4
                    word, lane = (x * TILE_Y + y) // 16, (x * TILE_Y + y) % 16
                    from_y = in_y[x, k] if y == 0 else before[b - 2]
                    if k == 1:
                        from_z = pltpu.roll(before[b - 1], 113, 1)
                    else:
                        from_z = pltpu.roll(z_in[word], 128 - lane, 1) if lane else z_in[word]
                    terms = []
                    for m in range(8):
                        q = (
                            rows[x, half, j, 8 + m : 9 + m, :] * before[b]
                            + rows[x, half, j, 16 + m : 17 + m, :] * from_y
                            + rows[x, half, j, 24 + m : 25 + m, :] * from_z
                        )
                        terms.append(pltpu.roll(q, 16 * m, 1) if m else q)
                    while len(terms) > 1:
                        terms = [u + v for u, v in zip(terms[::2], terms[1::2])]
                    partial = rows[x, half, j, 0:8, :] - terms[0]
                    high = partial.astype(jnp.bfloat16).astype(jnp.float32)
                    both = jnp.concatenate([high, partial - high], axis=0).astype(jnp.bfloat16)
                    product = jnp.dot(
                        both, weights[x, half, j], preferred_element_type=jnp.float32
                    )
                    solved = (product[0:8, 0:128] + product[8:16, 0:128]) + (
                        product[0:8, 128:256] + product[8:16, 128:256]
                    )
                    tile[x, half, j] = solved
                    done[b] = solved
                    if y == TILE_Y - 1:
                        out_y[x, k] = solved
                    if k == 1:
                        kept = jnp.where(last_lane, solved, 0.0)
                        z_out[word] = z_out[word] + pltpu.roll(kept, (lane + 113) % 128, 1)
        for b in range(2 * TILE_Y):
            out_x[b] = done[b]
        for h in range(2):
            out_z[h] = z_out[h]


def unpack_kernel(parts, out):
    odd = lax.rem(lax.axis_index("gx") // TILE_X, 2)
    senders = [2 * (OWNERS[0] + 2 * (odd ^ (s % 2))) + s // 2 for s in range(4)]
    for y in range(2):
        for n in range(8):
            rows = jnp.concatenate(
                [
                    parts[senders[s // 2], y * 2 + s % 2, n : n + 1, :]
                    for s in range(8)
                ],
                axis=0,
            )
            out[y, n] = swap_groups(rows)


def f32(*shape):
    return jax.ShapeDtypeStruct(shape, jnp.float32)


def local(right_side, inverse_blocks, couple_x, couple_y, couple_z):
    nx, ny = lax.axis_size("gx"), lax.axis_size("gy")
    outs = pl.pallas_call(
        pack_kernel,
        out_shape=[f32(4, 160, 128)] * 2 + [f32(2, 4, 160, 128)],
        in_specs=[HBM] * 5,
        out_specs=[VMEM] * 3,
        scratch_shapes=[
            pltpu.VMEM((2, 8, 32, 128), jnp.float32),
            pltpu.VMEM((2, 8, 8, 128), jnp.float32),
            pltpu.VMEM((2, 8, 128, 128), jnp.float32),
            pltpu.VMEM((2, 8, 8, 128), jnp.float32),
            pltpu.VMEM((2, 8, 8, 128), jnp.float32),
            pltpu.VMEM((128, 8), jnp.float32),
            pltpu.SemaphoreType.DMA((5,)),
        ],
        compiler_params=pltpu.CompilerParams(vmem_limit_bytes=12 << 20),
        name="pack",
    )(
        *(
            pltpu.with_memory_space_constraint(source, pltpu.HBM)
            for source in (
                right_side[0],
                inverse_blocks[0],
                couple_x[0],
                couple_y[0],
                couple_z.reshape(128, 8),
            )
        )
    )

    def device(gx, gy):
        return gx * ny + gy

    owners = [(gx, gy) for gx in range(nx) for gy in range(ny) if gx % TILE_X in OWNERS]
    everyone = [(gx, gy) for gx in range(nx) for gy in range(ny)]
    swap = [(device(gx, gy), device(gx ^ 1, gy)) for gx, gy in everyone]
    got = lax.ppermute(outs[2], AXES, swap)
    messages = [jnp.stack([outs[i], got[i]]) for i in range(2)]
    parts = [messages[0]]
    for across, along in ROUNDS[1:]:
        pairs = [
            (device((gx ^ 2 * along) + along // 2, gy ^ across), device(gx, gy))
            for gx, gy in owners
        ]
        parts.append(lax.ppermute(messages[across], AXES, pairs))
    weights, rows = pl.pallas_call(
        prepare_kernel,
        out_shape=[
            jax.ShapeDtypeStruct((TILE_X, 2, 4, 128, 256), jnp.bfloat16),
            f32(TILE_X, 2, 4, 32, 128),
        ],
        in_specs=[VMEM] * len(ROUNDS),
        out_specs=[VMEM] * 2,
        compiler_params=pltpu.CompilerParams(vmem_limit_bytes=16 << 20),
        name="prepare",
    )(*parts)

    steps = nx // TILE_X + ny // 2 + 4 - 2
    tile = jnp.zeros((TILE_X, 2, 4, 8, 128), jnp.float32)
    in_x = jnp.zeros((2 * TILE_Y, 8, 128), jnp.float32)
    in_y = jnp.zeros((TILE_X, 2, 8, 128), jnp.float32)
    in_z = jnp.zeros((2, 8, 128), jnp.float32)
    for step in range(steps):

        def body(*refs, step=step):
            step_kernel(step, *refs)

        tile, out_x, out_y, out_z = pl.pallas_call(
            body,
            out_shape=[f32(*tile.shape), f32(*in_x.shape), f32(*in_y.shape), f32(*in_z.shape)],
            in_specs=[VMEM] * 6,
            out_specs=[VMEM] * 4,
            input_output_aliases={5: 0},
            compiler_params=pltpu.CompilerParams(vmem_limit_bytes=12 << 20),
            name="tile_step",
        )(weights, rows, in_x, in_y, in_z, tile)
        if step == steps - 1:
            break
        to_x, to_y, to_z = [], [], []
        for gx, gy in owners:
            if tile_level(gx, gy) % REPEAT != step % REPEAT:
                continue
            here = device(gx, gy)
            other = gx // TILE_X * TILE_X + sum(OWNERS) - gx % TILE_X
            if gx + TILE_X < nx:
                to_x.append((here, device(other + TILE_X, gy)))
            if gy + 2 < ny:
                to_y.append((here, device(gx, gy + 2)))
            if (gx % TILE_X == OWNERS[0]) == (gx // TILE_X % 2 == 0):
                to_z.append((here, device(other, gy)))
            elif gy % 2 == 0:
                to_z.append((here, device(other, gy + 1)))
        in_x = lax.ppermute(out_x, AXES, to_x)
        in_y = lax.ppermute(out_y, AXES, to_y)
        in_z = lax.ppermute(out_z, AXES, to_z)

    groups = [
        [device(gx + i, gy + j) for i in range(TILE_X) for j in range(2)]
        for gx in range(0, nx, TILE_X)
        for gy in range(0, ny, 2)
    ]
    parts = lax.all_to_all(
        tile.reshape(MEMBERS, 4, 8, 128), AXES, 0, 0, axis_index_groups=groups, tiled=True
    )
    result = pl.pallas_call(
        unpack_kernel,
        out_shape=f32(2, 8, 8, 128),
        in_specs=[VMEM],
        out_specs=VMEM,
        name="unpack",
    )(parts)
    return result[None]


def solution(mesh):
    spec = P("gx", "gy", None, None, None)
    return jax.shard_map(
        local, mesh=mesh, in_specs=(spec,) * 5, out_specs=spec, check_vma=False
    )
```

```python
import jax
import jax.numpy as jnp
from jax import lax
from jax.experimental import pallas as pl
from jax.experimental.pallas import tpu as pltpu
from jax.sharding import PartitionSpec as P

AXES = ("gx", "gy")
TILE_X = 8
TILE_Y = 4
MEMBERS = 16
ROUNDS = ((0, 0), (1, 0), (1, 1), (1, 2), (1, 3), (0, 2), (0, 3), (0, 1))
SENT_X = 17
OWNERS = (2, 4)
REPEAT = 8
VMEM = pl.BlockSpec(memory_space=pltpu.VMEM)
HBM = pl.BlockSpec(memory_space=pltpu.HBM)


def swap_groups(a):
    row = lax.broadcasted_iota(jnp.int32, a.shape, 0)
    group = lax.broadcasted_iota(jnp.int32, a.shape, 1) // 16
    ahead = (group - row) & 7
    out = a
    for d in range(1, 8):
        moved = pltpu.roll(pltpu.roll(a, 8 - d, 0), 16 * d, 1)
        out = jnp.where(ahead == d, moved, out)
    return out


def pack_kernel(*refs):
    sources, outs, small, held, arrived = refs[:5], refs[5:8], refs[8], refs[9:14], refs[14]
    copies = [
        pltpu.make_async_copy(source, target, arrived.at[i])
        for i, (source, target) in enumerate(zip(sources, held))
    ]
    for copy in copies:
        copy.start()
    for copy in copies:
        copy.wait()
    rhs, inverse, cx, cy, cz = held
    gx = lax.axis_index("gx")
    core = lax.rem(gx, 2)
    pair = (lax.rem(gx, TILE_X) // 4) ^ lax.rem(gx // TILE_X, 2)
    upper = lax.rem(lax.axis_index("gy"), 2)
    row = lax.broadcasted_iota(jnp.int32, (8, 128), 0)
    group = lax.broadcasted_iota(jnp.int32, (8, 128), 1) // 16
    spread_row = lax.broadcasted_iota(jnp.int32, (8, 128), 0)
    spread_lane = lax.broadcasted_iota(jnp.int32, (8, 128), 1)
    spread = jnp.where(spread_lane == 16 * spread_row, 1.0, 0.0)
    heads = jnp.dot(
        cz[...], spread, precision=lax.Precision.HIGHEST, preferred_element_type=jnp.float32
    )
    for y in range(2):
        for n in range(8):
            small[y, :, n, :] = swap_groups(rhs[y, n])
        for ref, base in ((cx, 8), (cy, 16)):
            for m in range(8):
                a = ref[y, m]
                for c in range(8):
                    if c != m:
                        a = jnp.where(row == (c - m) % 8, ref[y, c], a)
                small[y, :, base + m, :] = swap_groups(a)
        for s in range(8):
            t = heads[(y * 8 + s) * 8 : (y * 8 + s + 1) * 8]
            out = t
            for d in range(1, 8):
                out = jnp.where(group == d, pltpu.roll(t, 8 - d, 0), out)
            small[y, s, 24:32, :] = out
    for across in range(2):
        for given in range(2):
            out = outs[2].at[across] if given else outs[across]
            first = 4 * (upper ^ across) + 2 * (pair ^ core ^ given)
            for y in range(2):
                for k in range(2):
                    out[y * 2 + k, 0:128, :] = inverse[y, first + k].T
                    out[y * 2 + k, 128:160, :] = small[y, first + k]


def prepare_kernel(*refs):
    parts, (weights, rows) = refs[: len(ROUNDS)], refs[len(ROUNDS) :]
    chip = lax.rem(lax.axis_index("gx"), TILE_X) // 2
    upper = lax.rem(lax.axis_index("gy"), 2)
    for part, (across, along) in zip(parts, ROUNDS):
        for i in range(2):
            x, half = 2 * (chip ^ along) + (i ^ (along // 2)), upper ^ across
            for b in range(4):
                full = part[i, b, 0:128, :]
                high = full.astype(jnp.bfloat16)
                low = (full - high.astype(jnp.float32)).astype(jnp.bfloat16)
                weights[x, half, b, :, 0:128] = high
                weights[x, half, b, :, 128:256] = low
                rows[x, half, b] = part[i, b, 128:160, :]


def tile_level(gx, gy):
    return gx // TILE_X + gy // 2 + 2 * (gy % 2) + ((gx % TILE_X) // 4 ^ (gx // TILE_X % 2))


def step_kernel(step, weights, rows, in_x, in_y, in_z, _, tile, out_x, out_y, out_z):
    gx, gy = lax.axis_index("gx"), lax.axis_index("gy")
    place = lax.rem(gx, TILE_X)
    owner = (place == OWNERS[0]) | (place == OWNERS[1])
    pair = (place // 4) ^ lax.rem(gx // TILE_X, 2)
    level = gx // TILE_X + gy // 2 + 2 * lax.rem(gy, 2) + pair
    last_lane = lax.rem(lax.broadcasted_iota(jnp.int32, (8, 128), 1), 16) == 15

    @pl.when(owner & (level == step))
    def _():
        z_in = [in_z[h] for h in range(2)]
        z_out = [jnp.zeros((8, 128), jnp.float32) for h in range(2)]
        done = [in_x[b] for b in range(2 * TILE_Y)]
        for i in range(TILE_X + TILE_Y):
            before = list(done)
            for y in range(TILE_Y):
                for k in range(2):
                    b, x = y * 2 + k, i - y - k
                    if not 0 <= x < TILE_X:
                        continue
                    half, j = b // 4, b % 4
                    word, lane = (x * TILE_Y + y) // 16, (x * TILE_Y + y) % 16
                    from_y = in_y[x, k] if y == 0 else before[b - 2]
                    if k == 1:
                        from_z = pltpu.roll(before[b - 1], 113, 1)
                    else:
                        from_z = pltpu.roll(z_in[word], 128 - lane, 1) if lane else z_in[word]
                    terms = []
                    for m in range(8):
                        q = (
                            rows[x, half, j, 8 + m : 9 + m, :] * before[b]
                            + rows[x, half, j, 16 + m : 17 + m, :] * from_y
                            + rows[x, half, j, 24 + m : 25 + m, :] * from_z
                        )
                        terms.append(pltpu.roll(q, 16 * m, 1) if m else q)
                    while len(terms) > 1:
                        terms = [u + v for u, v in zip(terms[::2], terms[1::2])]
                    partial = rows[x, half, j, 0:8, :] - terms[0]
                    high = partial.astype(jnp.bfloat16).astype(jnp.float32)
                    both = jnp.concatenate([high, partial - high], axis=0).astype(jnp.bfloat16)
                    product = jnp.dot(
                        both, weights[x, half, j], preferred_element_type=jnp.float32
                    )
                    solved = (product[0:8, 0:128] + product[8:16, 0:128]) + (
                        product[0:8, 128:256] + product[8:16, 128:256]
                    )
                    tile[x, half, j] = solved
                    done[b] = solved
                    if y == TILE_Y - 1:
                        out_y[x, k] = solved
                    if k == 1:
                        kept = jnp.where(last_lane, solved, 0.0)
                        z_out[word] = z_out[word] + pltpu.roll(kept, (lane + 113) % 128, 1)
        for b in range(2 * TILE_Y):
            out_x[b] = done[b]
        for h in range(2):
            out_z[h] = z_out[h]


def unpack_kernel(parts, out, blocks):
    odd = lax.rem(lax.axis_index("gx") // TILE_X, 2)
    senders = [2 * (OWNERS[0] + 2 * (odd ^ (s % 2))) + s // 2 for s in range(4)]
    for y in range(2):
        for s in range(8):
            blocks[y, s] = parts[senders[s // 2], y * 2 + s % 2]
    for y in range(2):
        for n in range(8):
            out[y, n] = swap_groups(blocks[y, :, n, :])


def f32(*shape):
    return jax.ShapeDtypeStruct(shape, jnp.float32)


def local(right_side, inverse_blocks, couple_x, couple_y, couple_z):
    nx, ny = lax.axis_size("gx"), lax.axis_size("gy")
    outs = pl.pallas_call(
        pack_kernel,
        out_shape=[f32(4, 160, 128)] * 2 + [f32(2, 4, 160, 128)],
        in_specs=[HBM] * 5,
        out_specs=[VMEM] * 3,
        scratch_shapes=[
            pltpu.VMEM((2, 8, 32, 128), jnp.float32),
            pltpu.VMEM((2, 8, 8, 128), jnp.float32),
            pltpu.VMEM((2, 8, 128, 128), jnp.float32),
            pltpu.VMEM((2, 8, 8, 128), jnp.float32),
            pltpu.VMEM((2, 8, 8, 128), jnp.float32),
            pltpu.VMEM((128, 8), jnp.float32),
            pltpu.SemaphoreType.DMA((5,)),
        ],
        compiler_params=pltpu.CompilerParams(vmem_limit_bytes=12 << 20),
        name="pack",
    )(
        *(
            pltpu.with_memory_space_constraint(source, pltpu.HBM)
            for source in (
                right_side[0],
                inverse_blocks[0],
                couple_x[0],
                couple_y[0],
                couple_z.reshape(128, 8),
            )
        )
    )

    def device(gx, gy):
        return gx * ny + gy

    owners = [(gx, gy) for gx in range(nx) for gy in range(ny) if gx % TILE_X in OWNERS]
    everyone = [(gx, gy) for gx in range(nx) for gy in range(ny)]
    swap = [(device(gx, gy), device(gx ^ 1, gy)) for gx, gy in everyone]
    got = lax.ppermute(outs[2], AXES, swap)
    messages = [jnp.stack([outs[i], got[i]]) for i in range(2)]
    parts = [messages[0]]
    for across, along in ROUNDS[1:]:
        pairs = [
            (device((gx ^ 2 * along) + along // 2, gy ^ across), device(gx, gy))
            for gx, gy in owners
        ]
        parts.append(lax.ppermute(messages[across], AXES, pairs))
    weights, rows = pl.pallas_call(
        prepare_kernel,
        out_shape=[
            jax.ShapeDtypeStruct((TILE_X, 2, 4, 128, 256), jnp.bfloat16),
            f32(TILE_X, 2, 4, 32, 128),
        ],
        in_specs=[VMEM] * len(ROUNDS),
        out_specs=[VMEM] * 2,
        compiler_params=pltpu.CompilerParams(vmem_limit_bytes=16 << 20),
        name="prepare",
    )(*parts)

    steps = nx // TILE_X + ny // 2 + 4 - 2
    tile = jnp.zeros((TILE_X, 2, 4, 8, 128), jnp.float32)
    in_x = jnp.zeros((SENT_X, 8, 128), jnp.float32)
    in_y = jnp.zeros((TILE_X, 2, 8, 128), jnp.float32)
    in_z = jnp.zeros((2, 8, 128), jnp.float32)
    for step in range(steps):

        def body(*refs, step=step):
            step_kernel(step, *refs)

        tile, out_x, out_y, out_z = pl.pallas_call(
            body,
            out_shape=[f32(*tile.shape), f32(*in_x.shape), f32(*in_y.shape), f32(*in_z.shape)],
            in_specs=[VMEM] * 6,
            out_specs=[VMEM] * 4,
            input_output_aliases={5: 0},
            compiler_params=pltpu.CompilerParams(vmem_limit_bytes=12 << 20),
            name="tile_step",
        )(weights, rows, in_x, in_y, in_z, tile)
        if step == steps - 1:
            break
        to_x, to_y, to_z = [], [], []
        for gx, gy in owners:
            if tile_level(gx, gy) % REPEAT != step % REPEAT:
                continue
            here = device(gx, gy)
            other = gx // TILE_X * TILE_X + sum(OWNERS) - gx % TILE_X
            if gx + TILE_X < nx:
                to_x.append((here, device(other + TILE_X, gy)))
            if gy + 2 < ny:
                to_y.append((here, device(gx, gy + 2)))
            if (gx % TILE_X == OWNERS[0]) == (gx // TILE_X % 2 == 0):
                to_z.append((here, device(other, gy)))
            elif gy % 2 == 0:
                to_z.append((here, device(other, gy + 1)))
        in_x = lax.ppermute(out_x, AXES, to_x)
        in_y = lax.ppermute(out_y, AXES, to_y)
        in_z = lax.ppermute(out_z, AXES, to_z)

    groups = [
        [device(gx + i, gy + j) for i in range(TILE_X) for j in range(2)]
        for gx in range(0, nx, TILE_X)
        for gy in range(0, ny, 2)
    ]
    parts = lax.all_to_all(
        tile.reshape(MEMBERS, 4, 8, 128), AXES, 0, 0, axis_index_groups=groups, tiled=True
    )
    result = pl.pallas_call(
        unpack_kernel,
        out_shape=f32(2, 8, 8, 128),
        in_specs=[VMEM],
        out_specs=VMEM,
        scratch_shapes=[pltpu.VMEM((2, 8, 8, 128), jnp.float32)],
        name="unpack",
    )(parts)
    return result[None]


def solution(mesh):
    spec = P("gx", "gy", None, None, None)
    return jax.shard_map(
        local, mesh=mesh, in_specs=(spec,) * 5, out_specs=spec, check_vma=False
    )
```

```python
import jax
import jax.numpy as jnp
from jax import lax
from jax.experimental import pallas as pl
from jax.experimental.pallas import tpu as pltpu
from jax.sharding import PartitionSpec as P

AXES = ("gx", "gy")
TILE_X = 8
TILE_Y = 4
MEMBERS = 16
ROUNDS = ((0, 0), (1, 0), (1, 1), (1, 3), (0, 3), (0, 1), (1, 2), (0, 2))
SENT_X = 17
OWNERS = (2, 4)
REPEAT = 8
VMEM = pl.BlockSpec(memory_space=pltpu.VMEM)
HBM = pl.BlockSpec(memory_space=pltpu.HBM)


def swap_groups(a):
    row = lax.broadcasted_iota(jnp.int32, a.shape, 0)
    group = lax.broadcasted_iota(jnp.int32, a.shape, 1) // 16
    ahead = (group - row) & 7
    out = a
    for d in range(1, 8):
        moved = pltpu.roll(pltpu.roll(a, 8 - d, 0), 16 * d, 1)
        out = jnp.where(ahead == d, moved, out)
    return out


def pack_kernel(*refs):
    sources, outs, small, held, arrived = refs[:5], refs[5:8], refs[8], refs[9:14], refs[14]
    copies = [
        pltpu.make_async_copy(source, target, arrived.at[i])
        for i, (source, target) in enumerate(zip(sources, held))
    ]
    for copy in copies:
        copy.start()
    for i in (0, 2, 3, 4):
        copies[i].wait()
    rhs, inverse, cx, cy, cz = held
    gx = lax.axis_index("gx")
    core = lax.rem(gx, 2)
    pair = (lax.rem(gx, TILE_X) // 4) ^ lax.rem(gx // TILE_X, 2)
    upper = lax.rem(lax.axis_index("gy"), 2)
    row = lax.broadcasted_iota(jnp.int32, (8, 128), 0)
    group = lax.broadcasted_iota(jnp.int32, (8, 128), 1) // 16
    spread_row = lax.broadcasted_iota(jnp.int32, (8, 128), 0)
    spread_lane = lax.broadcasted_iota(jnp.int32, (8, 128), 1)
    spread = jnp.where(spread_lane == 16 * spread_row, 1.0, 0.0)
    heads = jnp.dot(
        cz[...], spread, precision=lax.Precision.HIGHEST, preferred_element_type=jnp.float32
    )
    for y in range(2):
        for n in range(8):
            small[y, :, n, :] = swap_groups(rhs[y, n])
        for ref, base in ((cx, 8), (cy, 16)):
            for m in range(8):
                a = ref[y, m]
                for c in range(8):
                    if c != m:
                        a = jnp.where(row == (c - m) % 8, ref[y, c], a)
                small[y, :, base + m, :] = swap_groups(a)
        for s in range(8):
            t = heads[(y * 8 + s) * 8 : (y * 8 + s + 1) * 8]
            out = t
            for d in range(1, 8):
                out = jnp.where(group == d, pltpu.roll(t, 8 - d, 0), out)
            small[y, s, 24:32, :] = out
    copies[1].wait()
    for across in range(2):
        for given in range(2):
            out = outs[2].at[across] if given else outs[across]
            first = 4 * (upper ^ across) + 2 * (pair ^ core ^ given)
            for y in range(2):
                for k in range(2):
                    out[y * 2 + k, 0:128, :] = inverse[y, first + k].T
                    out[y * 2 + k, 128:160, :] = small[y, first + k]


def prepare_kernel(*refs):
    parts, (weights, rows) = refs[: len(ROUNDS)], refs[len(ROUNDS) :]
    chip = lax.rem(lax.axis_index("gx"), TILE_X) // 2
    upper = lax.rem(lax.axis_index("gy"), 2)
    for part, (across, along) in zip(parts, ROUNDS):
        for i in range(2):
            x, half = 2 * (chip ^ along) + (i ^ (along // 2)), upper ^ across
            for b in range(4):
                full = part[i, b, 0:128, :]
                high = full.astype(jnp.bfloat16)
                low = (full - high.astype(jnp.float32)).astype(jnp.bfloat16)
                weights[x, half, b, :, 0:128] = high
                weights[x, half, b, :, 128:256] = low
                rows[x, half, b] = part[i, b, 128:160, :]


def tile_level(gx, gy):
    return gx // TILE_X + gy // 2 + 2 * (gy % 2) + ((gx % TILE_X) // 4 ^ (gx // TILE_X % 2))


def step_kernel(step, weights, rows, in_x, in_y, in_z, _, tile, out_x, out_y, out_z):
    gx, gy = lax.axis_index("gx"), lax.axis_index("gy")
    place = lax.rem(gx, TILE_X)
    owner = (place == OWNERS[0]) | (place == OWNERS[1])
    pair = (place // 4) ^ lax.rem(gx // TILE_X, 2)
    level = gx // TILE_X + gy // 2 + 2 * lax.rem(gy, 2) + pair
    last_lane = lax.rem(lax.broadcasted_iota(jnp.int32, (8, 128), 1), 16) == 15

    @pl.when(owner & (level == step))
    def _():
        z_in = [in_z[h] for h in range(2)]
        z_out = [jnp.zeros((8, 128), jnp.float32) for h in range(2)]
        done = [in_x[b] for b in range(2 * TILE_Y)]
        for i in range(TILE_X + TILE_Y):
            before = list(done)
            for y in range(TILE_Y):
                for k in range(2):
                    b, x = y * 2 + k, i - y - k
                    if not 0 <= x < TILE_X:
                        continue
                    half, j = b // 4, b % 4
                    word, lane = (x * TILE_Y + y) // 16, (x * TILE_Y + y) % 16
                    from_y = in_y[x, k] if y == 0 else before[b - 2]
                    if k == 1:
                        from_z = pltpu.roll(before[b - 1], 113, 1)
                    else:
                        from_z = pltpu.roll(z_in[word], 128 - lane, 1) if lane else z_in[word]
                    terms = []
                    for m in range(8):
                        q = (
                            rows[x, half, j, 8 + m : 9 + m, :] * before[b]
                            + rows[x, half, j, 16 + m : 17 + m, :] * from_y
                            + rows[x, half, j, 24 + m : 25 + m, :] * from_z
                        )
                        terms.append(pltpu.roll(q, 16 * m, 1) if m else q)
                    while len(terms) > 1:
                        terms = [u + v for u, v in zip(terms[::2], terms[1::2])]
                    partial = rows[x, half, j, 0:8, :] - terms[0]
                    high = partial.astype(jnp.bfloat16).astype(jnp.float32)
                    both = jnp.concatenate([high, partial - high], axis=0).astype(jnp.bfloat16)
                    product = jnp.dot(
                        both, weights[x, half, j], preferred_element_type=jnp.float32
                    )
                    solved = (product[0:8, 0:128] + product[8:16, 0:128]) + (
                        product[0:8, 128:256] + product[8:16, 128:256]
                    )
                    tile[x, half, j] = solved
                    done[b] = solved
                    if y == TILE_Y - 1:
                        out_y[x, k] = solved
                    if k == 1:
                        kept = jnp.where(last_lane, solved, 0.0)
                        z_out[word] = z_out[word] + pltpu.roll(kept, (lane + 113) % 128, 1)
        for b in range(2 * TILE_Y):
            out_x[b] = done[b]
        for h in range(2):
            out_z[h] = z_out[h]


def unpack_kernel(parts, out, blocks):
    odd = lax.rem(lax.axis_index("gx") // TILE_X, 2)
    senders = [2 * (OWNERS[0] + 2 * (odd ^ (s % 2))) + s // 2 for s in range(4)]
    for y in range(2):
        for s in range(8):
            blocks[y, s] = parts[senders[s // 2], y * 2 + s % 2]
    for y in range(2):
        for n in range(8):
            out[y, n] = swap_groups(blocks[y, :, n, :])


def f32(*shape):
    return jax.ShapeDtypeStruct(shape, jnp.float32)


def local(right_side, inverse_blocks, couple_x, couple_y, couple_z):
    nx, ny = lax.axis_size("gx"), lax.axis_size("gy")
    outs = pl.pallas_call(
        pack_kernel,
        out_shape=[f32(4, 160, 128)] * 2 + [f32(2, 4, 160, 128)],
        in_specs=[HBM] * 5,
        out_specs=[VMEM] * 3,
        scratch_shapes=[
            pltpu.VMEM((2, 8, 32, 128), jnp.float32),
            pltpu.VMEM((2, 8, 8, 128), jnp.float32),
            pltpu.VMEM((2, 8, 128, 128), jnp.float32),
            pltpu.VMEM((2, 8, 8, 128), jnp.float32),
            pltpu.VMEM((2, 8, 8, 128), jnp.float32),
            pltpu.VMEM((128, 8), jnp.float32),
            pltpu.SemaphoreType.DMA((5,)),
        ],
        compiler_params=pltpu.CompilerParams(vmem_limit_bytes=12 << 20),
        name="pack",
    )(
        *(
            pltpu.with_memory_space_constraint(source, pltpu.HBM)
            for source in (
                right_side[0],
                inverse_blocks[0],
                couple_x[0],
                couple_y[0],
                couple_z.reshape(128, 8),
            )
        )
    )

    def device(gx, gy):
        return gx * ny + gy

    owners = [(gx, gy) for gx in range(nx) for gy in range(ny) if gx % TILE_X in OWNERS]
    everyone = [(gx, gy) for gx in range(nx) for gy in range(ny)]
    swap = [(device(gx, gy), device(gx ^ 1, gy)) for gx, gy in everyone]
    got = lax.ppermute(outs[2], AXES, swap)
    messages = [jnp.stack([outs[i], got[i]]) for i in range(2)]
    parts = [messages[0]]
    for across, along in ROUNDS[1:]:
        pairs = [
            (device((gx ^ 2 * along) + along // 2, gy ^ across), device(gx, gy))
            for gx, gy in owners
        ]
        message = messages[across]
        if along == 2:
            message, _ = lax.optimization_barrier((message, parts[1 + (across == 0)]))
        parts.append(lax.ppermute(message, AXES, pairs))
    weights, rows = pl.pallas_call(
        prepare_kernel,
        out_shape=[
            jax.ShapeDtypeStruct((TILE_X, 2, 4, 128, 256), jnp.bfloat16),
            f32(TILE_X, 2, 4, 32, 128),
        ],
        in_specs=[VMEM] * len(ROUNDS),
        out_specs=[VMEM] * 2,
        compiler_params=pltpu.CompilerParams(vmem_limit_bytes=16 << 20),
        name="prepare",
    )(*parts)

    steps = nx // TILE_X + ny // 2 + 4 - 2
    tile = jnp.zeros((TILE_X, 2, 4, 8, 128), jnp.float32)
    in_x = jnp.zeros((SENT_X, 8, 128), jnp.float32)
    in_y = jnp.zeros((TILE_X, 2, 8, 128), jnp.float32)
    in_z = jnp.zeros((2, 8, 128), jnp.float32)
    for step in range(steps):

        def body(*refs, step=step):
            step_kernel(step, *refs)

        tile, out_x, out_y, out_z = pl.pallas_call(
            body,
            out_shape=[f32(*tile.shape), f32(*in_x.shape), f32(*in_y.shape), f32(*in_z.shape)],
            in_specs=[VMEM] * 6,
            out_specs=[VMEM] * 4,
            input_output_aliases={5: 0},
            compiler_params=pltpu.CompilerParams(vmem_limit_bytes=12 << 20),
            name="tile_step",
        )(weights, rows, in_x, in_y, in_z, tile)
        if step == steps - 1:
            break
        to_x, to_y, to_z = [], [], []
        for gx, gy in owners:
            if tile_level(gx, gy) % REPEAT != step % REPEAT:
                continue
            here = device(gx, gy)
            other = gx // TILE_X * TILE_X + sum(OWNERS) - gx % TILE_X
            if gx + TILE_X < nx:
                to_x.append((here, device(other + TILE_X, gy)))
            if gy + 2 < ny:
                to_y.append((here, device(gx, gy + 2)))
            if (gx % TILE_X == OWNERS[0]) == (gx // TILE_X % 2 == 0):
                to_z.append((here, device(other, gy)))
            elif gy % 2 == 0:
                to_z.append((here, device(other, gy + 1)))
        in_x = lax.ppermute(out_x, AXES, to_x)
        in_y = lax.ppermute(out_y, AXES, to_y)
        in_z = lax.ppermute(out_z, AXES, to_z)

    groups = [
        [device(gx + i, gy + j) for i in range(TILE_X) for j in range(2)]
        for gx in range(0, nx, TILE_X)
        for gy in range(0, ny, 2)
    ]
    parts = lax.all_to_all(
        tile.reshape(MEMBERS, 4, 8, 128), AXES, 0, 0, axis_index_groups=groups, tiled=True
    )
    result = pl.pallas_call(
        unpack_kernel,
        out_shape=f32(2, 8, 8, 128),
        in_specs=[VMEM],
        out_specs=VMEM,
        scratch_shapes=[pltpu.VMEM((2, 8, 8, 128), jnp.float32)],
        name="unpack",
    )(parts)
    return result[None]


def solution(mesh):
    spec = P("gx", "gy", None, None, None)
    return jax.shard_map(
        local, mesh=mesh, in_specs=(spec,) * 5, out_specs=spec, check_vma=False
    )
```

```python
import jax
import jax.numpy as jnp
from jax import lax
from jax.experimental import pallas as pl
from jax.experimental.pallas import tpu as pltpu
from jax.sharding import PartitionSpec as P

AXES = ("gx", "gy")
TILE_X = 8
TILE_Y = 4
MEMBERS = 16
ROUNDS = ((0, 0), (1, 0), (1, 1), (1, 3), (0, 3), (0, 1), (1, 2), (0, 2))
SENT_X = 17
OWNERS = (2, 4)
REPEAT = 8
VMEM = pl.BlockSpec(memory_space=pltpu.VMEM)
HBM = pl.BlockSpec(memory_space=pltpu.HBM)


def swap_groups(a):
    row = lax.broadcasted_iota(jnp.int32, a.shape, 0)
    group = lax.broadcasted_iota(jnp.int32, a.shape, 1) // 16
    ahead = (group - row) & 7
    out = a
    for d in range(1, 8):
        moved = pltpu.roll(pltpu.roll(a, 8 - d, 0), 16 * d, 1)
        out = jnp.where(ahead == d, moved, out)
    return out


def pack_kernel(*refs):
    sources, outs, small, held, arrived = refs[:5], refs[5:8], refs[8], refs[9:14], refs[14]
    copies = [
        pltpu.make_async_copy(source, target, arrived.at[i])
        for i, (source, target) in enumerate(zip(sources, held))
    ]
    for copy in copies:
        copy.start()
    for i in (0, 2, 3, 4):
        copies[i].wait()
    rhs, inverse, cx, cy, cz = held
    gx = lax.axis_index("gx")
    core = lax.rem(gx, 2)
    pair = (lax.rem(gx, TILE_X) // 4) ^ lax.rem(gx // TILE_X, 2)
    upper = lax.rem(lax.axis_index("gy"), 2)
    row = lax.broadcasted_iota(jnp.int32, (8, 128), 0)
    group = lax.broadcasted_iota(jnp.int32, (8, 128), 1) // 16
    spread_row = lax.broadcasted_iota(jnp.int32, (8, 128), 0)
    spread_lane = lax.broadcasted_iota(jnp.int32, (8, 128), 1)
    spread = jnp.where(spread_lane == 16 * spread_row, 1.0, 0.0)
    heads = jnp.dot(
        cz[...], spread, precision=lax.Precision.HIGHEST, preferred_element_type=jnp.float32
    )
    for y in range(2):
        for n in range(8):
            small[y, :, n, :] = swap_groups(rhs[y, n])
        for ref, base in ((cx, 8), (cy, 16)):
            for m in range(8):
                a = ref[y, m]
                for c in range(8):
                    if c != m:
                        a = jnp.where(row == (c - m) % 8, ref[y, c], a)
                small[y, :, base + m, :] = swap_groups(a)
        for s in range(8):
            t = heads[(y * 8 + s) * 8 : (y * 8 + s + 1) * 8]
            out = t
            for d in range(1, 8):
                out = jnp.where(group == d, pltpu.roll(t, 8 - d, 0), out)
            small[y, s, 24:32, :] = out
    copies[1].wait()
    for across in range(2):
        for given in range(2):
            out = outs[2].at[across] if given else outs[across]
            first = 4 * (upper ^ across) + 2 * (pair ^ core ^ given)
            for y in range(2):
                for k in range(2):
                    out[y * 2 + k, 0:128, :] = inverse[y, first + k].T
                    out[y * 2 + k, 128:160, :] = small[y, first + k]


def prepare_kernel(*refs):
    parts, (weights, rows) = refs[: len(ROUNDS)], refs[len(ROUNDS) :]
    chip = lax.rem(lax.axis_index("gx"), TILE_X) // 2
    upper = lax.rem(lax.axis_index("gy"), 2)
    for part, (across, along) in zip(parts, ROUNDS):
        for i in range(2):
            x, half = 2 * (chip ^ along) + (i ^ (along // 2)), upper ^ across
            for b in range(4):
                full = part[i, b, 0:128, :]
                high = full.astype(jnp.bfloat16)
                low = (full - high.astype(jnp.float32)).astype(jnp.bfloat16)
                weights[x, half, b, :, 0:128] = high
                weights[x, half, b, :, 128:256] = low
                rows[x, half, b] = part[i, b, 128:160, :]


def tile_level(gx, gy):
    return gx // TILE_X + gy // 2 + 2 * (gy % 2) + ((gx % TILE_X) // 4 ^ (gx // TILE_X % 2))


def step_kernel(step, weights, rows, in_x, in_y, in_z, _, tile, out_x, out_y, out_z):
    gx, gy = lax.axis_index("gx"), lax.axis_index("gy")
    place = lax.rem(gx, TILE_X)
    owner = (place == OWNERS[0]) | (place == OWNERS[1])
    pair = (place // 4) ^ lax.rem(gx // TILE_X, 2)
    level = gx // TILE_X + gy // 2 + 2 * lax.rem(gy, 2) + pair
    last_lane = lax.rem(lax.broadcasted_iota(jnp.int32, (8, 128), 1), 16) == 15

    @pl.when(owner & (level == step))
    def _():
        z_in = [in_z[h] for h in range(2)]
        z_out = [jnp.zeros((8, 128), jnp.float32) for h in range(2)]
        done = [in_x[b] for b in range(2 * TILE_Y)]
        for i in range(TILE_X + TILE_Y):
            before = list(done)
            for y in range(TILE_Y):
                for k in range(2):
                    b, x = y * 2 + k, i - y - k
                    if not 0 <= x < TILE_X:
                        continue
                    half, j = b // 4, b % 4
                    word, lane = (x * TILE_Y + y) // 16, (x * TILE_Y + y) % 16
                    from_y = in_y[x, k] if y == 0 else before[b - 2]
                    if k == 1:
                        from_z = pltpu.roll(before[b - 1], 113, 1)
                    else:
                        from_z = pltpu.roll(z_in[word], 128 - lane, 1) if lane else z_in[word]
                    terms = []
                    for m in range(8):
                        q = (
                            rows[x, half, j, 8 + m : 9 + m, :] * before[b]
                            + rows[x, half, j, 16 + m : 17 + m, :] * from_y
                            + rows[x, half, j, 24 + m : 25 + m, :] * from_z
                        )
                        terms.append(pltpu.roll(q, 16 * m, 1) if m else q)
                    while len(terms) > 1:
                        terms = [u + v for u, v in zip(terms[::2], terms[1::2])]
                    partial = rows[x, half, j, 0:8, :] - terms[0]
                    high = partial.astype(jnp.bfloat16).astype(jnp.float32)
                    both = jnp.concatenate([high, partial - high], axis=0).astype(jnp.bfloat16)
                    product = jnp.dot(
                        both, weights[x, half, j], preferred_element_type=jnp.float32
                    )
                    solved = (product[0:8, 0:128] + product[8:16, 0:128]) + (
                        product[0:8, 128:256] + product[8:16, 128:256]
                    )
                    tile[x, half, j] = solved
                    done[b] = solved
                    if y == TILE_Y - 1:
                        out_y[x, k] = solved
                    if k == 1:
                        kept = jnp.where(last_lane, solved, 0.0)
                        z_out[word] = z_out[word] + pltpu.roll(kept, (lane + 113) % 128, 1)
        for b in range(2 * TILE_Y):
            out_x[b] = done[b]
        for h in range(2):
            out_z[h] = z_out[h]


def unpack_kernel(parts, out, blocks):
    odd = lax.rem(lax.axis_index("gx") // TILE_X, 2)
    senders = [2 * (OWNERS[0] + 2 * (odd ^ (s % 2))) + s // 2 for s in range(4)]
    for y in range(2):
        for s in range(8):
            blocks[y, s] = parts[senders[s // 2], y * 2 + s % 2]
    for y in range(2):
        for n in range(8):
            out[y, n] = swap_groups(blocks[y, :, n, :])


def f32(*shape):
    return jax.ShapeDtypeStruct(shape, jnp.float32)


def local(right_side, inverse_blocks, couple_x, couple_y, couple_z):
    nx, ny = lax.axis_size("gx"), lax.axis_size("gy")
    outs = pl.pallas_call(
        pack_kernel,
        out_shape=[f32(4, 160, 128)] * 2 + [f32(2, 4, 160, 128)],
        in_specs=[HBM] * 5,
        out_specs=[VMEM] * 3,
        scratch_shapes=[
            pltpu.VMEM((2, 8, 32, 128), jnp.float32),
            pltpu.VMEM((2, 8, 8, 128), jnp.float32),
            pltpu.VMEM((2, 8, 128, 128), jnp.float32),
            pltpu.VMEM((2, 8, 8, 128), jnp.float32),
            pltpu.VMEM((2, 8, 8, 128), jnp.float32),
            pltpu.VMEM((128, 8), jnp.float32),
            pltpu.SemaphoreType.DMA((5,)),
        ],
        compiler_params=pltpu.CompilerParams(vmem_limit_bytes=12 << 20),
        name="pack",
    )(
        *(
            pltpu.with_memory_space_constraint(source, pltpu.HBM)
            for source in (
                right_side[0],
                inverse_blocks[0],
                couple_x[0],
                couple_y[0],
                couple_z.reshape(128, 8),
            )
        )
    )

    def device(gx, gy):
        return gx * ny + gy

    owners = [(gx, gy) for gx in range(nx) for gy in range(ny) if gx % TILE_X in OWNERS]
    everyone = [(gx, gy) for gx in range(nx) for gy in range(ny)]
    swap = [(device(gx, gy), device(gx ^ 1, gy)) for gx, gy in everyone]
    got = lax.ppermute(outs[2], AXES, swap)
    messages = [jnp.stack([outs[i], got[i]]) for i in range(2)]
    parts = [messages[0]]
    for across, along in ROUNDS[1:]:
        pairs = [
            (device((gx ^ 2 * along) + along // 2, gy ^ across), device(gx, gy))
            for gx, gy in owners
        ]
        message = messages[across]
        if along == 2:
            message, _ = lax.optimization_barrier((message, parts[1 + (across == 0)]))
        parts.append(lax.ppermute(message, AXES, pairs))
    weights, rows = pl.pallas_call(
        prepare_kernel,
        out_shape=[
            jax.ShapeDtypeStruct((TILE_X, 2, 4, 128, 256), jnp.bfloat16),
            f32(TILE_X, 2, 4, 32, 128),
        ],
        in_specs=[VMEM] * len(ROUNDS),
        out_specs=[VMEM] * 2,
        compiler_params=pltpu.CompilerParams(vmem_limit_bytes=16 << 20),
        name="prepare",
    )(*parts)

    steps = nx // TILE_X + ny // 2 + 4 - 2
    tile = jnp.zeros((TILE_X, 2, 4, 8, 128), jnp.float32)
    in_x = jnp.zeros((SENT_X, 8, 128), jnp.float32)
    in_y = jnp.zeros((TILE_X, 2, 8, 128), jnp.float32)
    in_z = jnp.zeros((2, 8, 128), jnp.float32)
    for step in range(steps):

        def body(*refs, step=step):
            step_kernel(step, *refs)

        tile, out_x, out_y, out_z = pl.pallas_call(
            body,
            out_shape=[f32(*tile.shape), f32(*in_x.shape), f32(*in_y.shape), f32(*in_z.shape)],
            in_specs=[VMEM] * 6,
            out_specs=[VMEM] * 4,
            input_output_aliases={5: 0},
            compiler_params=pltpu.CompilerParams(vmem_limit_bytes=12 << 20),
            name="tile_step",
        )(weights, rows, in_x, in_y, in_z, tile)
        if step == steps - 1:
            break
        to_x, to_y, to_z = [], [], []
        for gx, gy in owners:
            if tile_level(gx, gy) % REPEAT != step % REPEAT:
                continue
            here = device(gx, gy)
            other = gx // TILE_X * TILE_X + sum(OWNERS) - gx % TILE_X
            if gx + TILE_X < nx:
                to_x.append((here, device(other + TILE_X, gy)))
            if gy + 2 < ny:
                to_y.append((here, device(gx, gy + 2)))
            if (gx % TILE_X == OWNERS[0]) == (gx // TILE_X % 2 == 0):
                to_z.append((here, device(other, gy)))
            elif gy % 2 == 0:
                to_z.append((here, device(other, gy + 1)))
        in_x = lax.ppermute(out_x, AXES, to_x)
        in_y = lax.ppermute(out_y, AXES, to_y)
        in_z = lax.ppermute(out_z, AXES, to_z)

    groups = [
        [device(gx + i, gy + j) for i in range(TILE_X) for j in range(2)]
        for gx in range(0, nx, TILE_X)
        for gy in range(0, ny, 2)
    ]
    parts = lax.all_to_all(
        tile.reshape(MEMBERS, 4, 8, 128), AXES, 0, 0, axis_index_groups=groups, tiled=True
    )
    result = pl.pallas_call(
        unpack_kernel,
        out_shape=f32(2, 8, 8, 128),
        in_specs=[VMEM],
        out_specs=VMEM,
        scratch_shapes=[pltpu.VMEM((2, 8, 8, 128), jnp.float32)],
        compiler_params=pltpu.CompilerParams(vmem_limit_bytes=4 << 20),
        name="unpack",
    )(parts)
    return result[None]


def solution(mesh):
    spec = P("gx", "gy", None, None, None)
    return jax.shard_map(
        local, mesh=mesh, in_specs=(spec,) * 5, out_specs=spec, check_vma=False
    )
```
